128 devices in a mesh: section: 4 (over y), expert: 16 (over x, z_hi, core), dp: 2 (over z_lo).
Axes of the slice: x: 4, y: 4, z: 4 (z_hi: 2, z_lo: 2; z = z_hi * 2 + z_lo), core: 2. Of those that a mesh axis runs over, the one named last changes fastest.
Arguments:
- activations: bfloat16 [4, 4096, 4096], P('section', ('dp', 'expert')), parts along dimension 1, may hold values from -6 to 6
- routes: int32 [2, 4, 4096, 8], P(None, 'section', ('dp', 'expert')), parts along dimension 2, may hold values from 0 to 15, all different within a row; in each aligned block of 128 rows (0 to 127, 128 to 255, ..., all dimensions but the last counted through in order) at most 72 rows name the same one
- combine: float32 [2, 4, 4096, 8], P(None, 'section', ('dp', 'expert')), parts along dimension 2, may hold values from 0.2 to 1
- norm_gain: float32 [4, 4096], P('section'), may hold values from 0.5 to 2
- up_weight: bfloat16 [4, 16, 4096, 768], P('section', 'expert'), may hold values from -0.09375 to 0.09375
- down_weight: bfloat16 [4, 16, 768, 4096], P('section', 'expert'), may hold values from -0.21875 to 0.21875
Outputs:
- carried: bfloat16 [4, 4096, 4096], P('section', ('dp', 'expert')), parts along dimension 1
The draws below stay inside these ranges and needn't reach their ends.
There are 2 independent parts, one for each index of `dp`. The reference program is written for one: setup_inputs(seed, part) draws one part's arguments, and reference() takes and returns one part's arrays. A program takes and returns all parts, laid end to end along the dimension named above; an argument that names none is the same for every part. Nothing has to cross between parts.
Inputs may be any that keep to these rules, and one draw needn't show every extreme that they name: `routes`: in each aligned block of 128 rows (the rows of one device) no expert is named by more than 72 pairs; the ids of one row differ.
All inputs are finite; a program needn't handle non-finite values.
Results may differ from the reference program's by a relative error of at most 0.007.
Values may be sent and summed in bfloat16 or wider, within the bound.
No kernel may reach another device: no remote copies, remote signals or barrier semaphores. Data moves between devices by JAX's collectives and lax.ppermute only.
A program may use at most 128 MiB of HBM per device.

```python
import math
import jax
import jax.numpy as jnp
import numpy as np
from jax import lax

D = 4096
FE = 768
TOK_DEV = 128
STOPS = 2
TOP = 8
CAP = 72
ROWS = 2048
N_SECTION = 4
N_EXPERT = 16


def block_scale(own_key, extent, cuts, least, high):
    factor_of, own = 1.0, jax.random.fold_in(own_key, 6)
    for axis_at, shards_of in cuts:
        steps = jnp.exp(jax.random.uniform(jax.random.fold_in(own, axis_at), (shards_of,), jnp.float32, least / len(cuts), high / len(cuts)))
        factor_of = factor_of * jnp.repeat(steps, extent[axis_at] // shards_of).reshape([-1 if axis == axis_at else 1 for axis in range(len(extent))])
    return factor_of


def deal_out(key, own, number, rows, number_of, top, limit, lean):
    ranking = jax.random.permutation(key, number_of)
    crowded, usual = load_shares(number_of, rows * top, limit, lean, True), load_shares(number_of, rows * top, limit, lean, False)
    places = jnp.arange(number_of)

    def named(tallies, rotation):
        used = int((tallies > 0).sum())
        fixed = max(1, used // 4)
        passed = fixed + (places - fixed + rotation * (used - fixed)) % max(1, number_of - fixed)
        return jnp.zeros((number_of,), jnp.int32).at[ranking[jnp.where(places < fixed, places, passed)]].set(jnp.asarray(tallies, jnp.int32))

    tallies = jnp.where(number % 4 == 0, named(crowded, number // 4), named(usual, number - number // 4 - 1))
    mixed = jax.random.permutation(jax.random.fold_in(own, 3), number_of)
    giver, sink = mixed[0:number_of // 2 * 2:2], mixed[1:number_of // 2 * 2:2]
    slack = jnp.minimum(tallies[giver] - 1, limit - tallies[sink]) // 2
    slack = jnp.where((giver == ranking[0]) | (sink == ranking[0]) | (tallies[sink] == 0), 0, jnp.maximum(slack, 0))
    passed = jax.random.randint(jax.random.fold_in(own, 4), (number_of // 2,), 0, 1 << 20) % (slack + 1)
    tallies = tallies.at[giver].add(-passed).at[sink].add(passed)
    members = jnp.searchsorted(jnp.cumsum(tallies), jnp.arange(rows * top), side="right").astype(jnp.int32)
    grid = members.reshape(top, rows).T
    grid = grid[jax.random.permutation(jax.random.fold_in(own, 1), rows)]
    rotation = jax.random.randint(jax.random.fold_in(own, 2), (rows, 1), 0, top)
    return jnp.take_along_axis(grid, (jnp.arange(top)[None, :] + rotation) % top, axis=1)


def load_shares(count, total, limit, skew, full):
    loads = [(1 << 20) // math.isqrt(grade ** skew) + 1 for grade in range(1, count + 1)]
    largest = limit if full else min(limit, max(-(-total // count), total * loads[0] // sum(loads)))
    least = 1 if total - largest >= count - 1 else 0
    counts, rest = [largest] + [least] * (count - 1), total - largest - least * (count - 1)
    while rest > 0:
        candidates = [i for i in range(1, count) if counts[i] < largest] or [i for i in range(1, count) if counts[i] < limit]
        mass, budget = sum([loads[i] for i in candidates]), rest
        for i in candidates:
            extra = min(limit - counts[i], max(1, budget * loads[i] // mass), rest)
            counts[i] = counts[i] + extra
            rest = rest - extra
    return np.array(counts)


def centred(rng, dims, scale, limit, cuts=(), held_as=jnp.bfloat16):
    values = jax.random.normal(rng, dims, jnp.float32) * scale
    if len(cuts) > 0:
        values = block_scale(rng, dims, cuts, -0.22, 0.18) * values
    return jnp.clip(values, min=-limit, max=limit).astype(held_as)


def setup_inputs(seed: int = 0, part: int = 0) -> dict:
    keys = jax.random.split(jax.random.key(seed), 7)
    part_keys = jax.random.split(jax.random.fold_in(keys[6], part), 7)
    activations = centred(part_keys[0], (N_SECTION, ROWS, D), 1.0, 6.0, ((0, 4), (1, 16)))
    routes_keys = jax.random.split(jax.random.fold_in(part_keys[1], 1), STOPS * N_SECTION * ROWS // TOK_DEV)
    routes_turns = jax.random.permutation(jax.random.fold_in(part_keys[1], 3), STOPS * N_SECTION * ROWS // TOK_DEV)
    routes = jax.vmap(lambda own, number: deal_out(jax.random.fold_in(part_keys[1], 2), own, number, TOK_DEV, N_EXPERT, TOP, CAP, 2))(routes_keys, routes_turns).reshape((STOPS, N_SECTION, ROWS, TOP))
    combine = jnp.clip(0.2 + 0.8 * jax.random.uniform(part_keys[2], (STOPS, N_SECTION, ROWS, TOP), jnp.float32) ** block_scale(part_keys[2], (STOPS, N_SECTION, ROWS, TOP), ((1, 4), (2, 16)), -0.2, 0.2), 0.2, 1.0)
    norm_gain = jnp.clip(jnp.exp(math.log(2.0) - 1.3862944 * jax.random.uniform(keys[3], (N_SECTION, D), jnp.float32) ** block_scale(keys[3], (N_SECTION, D), ((0, 4),), -0.2, 0.2)), 0.5, 2.0)
    up_weight = centred(keys[4], (N_SECTION, N_EXPERT, D, FE), D ** -0.5, 0.09375, ((0, 4), (1, 16)))
    down_weight = centred(keys[5], (N_SECTION, N_EXPERT, FE, D), FE ** -0.5, 0.21875, ((0, 4), (1, 16)))
    return dict(activations=activations, routes=routes, combine=combine, norm_gain=norm_gain, up_weight=up_weight, down_weight=down_weight)


def slot_of(expert_ids):
    flattened = expert_ids.reshape(-1)
    onehot = (flattened[:, None] == jnp.arange(N_EXPERT, dtype=jnp.int32)[None, :]).astype(jnp.int32)
    before = jnp.cumsum(onehot, axis=0) - onehot
    return lax.optimization_barrier(jnp.sum(before * onehot, axis=1)).astype(jnp.int32).reshape(expert_ids.shape)

def section_stop(inputs):
    state, expert_ids, weights_now, gain_row, up_proj, down_proj = inputs
    wide_state = state.astype(jnp.float32)
    normed = (wide_state * lax.rsqrt(lax.optimization_barrier(jnp.mean(wide_state * wide_state, axis=-1, keepdims=True)) + 1e-06) * gain_row).astype(jnp.bfloat16)
    blocks = N_EXPERT
    block_ids = expert_ids.reshape(blocks, TOK_DEV, TOP)
    slots = jax.vmap(slot_of)(block_ids)
    block_rows = normed.reshape(blocks, TOK_DEV, D)
    block_index = jnp.arange(blocks, dtype=jnp.int32)[:, None, None]
    spread = jnp.broadcast_to(block_rows[:, :, None, :], (blocks, TOK_DEV, TOP, D))
    outbox = jnp.zeros((blocks, N_EXPERT, CAP, D), jnp.bfloat16).at[block_index, block_ids, slots].set(spread)

    def run_expert(args):
        arrived, up_one, down_one = args
        hidden = jax.nn.silu(jnp.dot(arrived.reshape(-1, D), up_one, preferred_element_type=jnp.float32)).astype(jnp.bfloat16)
        return jnp.dot(hidden, down_one, preferred_element_type=jnp.float32).astype(jnp.bfloat16).reshape(blocks, CAP, D)
    served = lax.map(run_expert, (jnp.transpose(outbox, (1, 0, 2, 3)), up_proj, down_proj))
    picked = served[block_ids, block_index, slots].astype(jnp.float32)
    summed = lax.optimization_barrier(jnp.sum(picked * weights_now.reshape(blocks, TOK_DEV, TOP)[..., None], axis=2))
    return (wide_state + summed.reshape(-1, D)).astype(jnp.bfloat16)

def reference(activations, routes, combine, norm_gain, up_weight, down_weight):
    state = activations
    for visit in range(STOPS):
        mixed = lax.map(section_stop, (state, routes[visit], combine[visit], norm_gain, up_weight, down_weight))
        state = jnp.roll(mixed, 1, axis=0)
    return state
```

```python
import functools

import jax
import jax.numpy as jnp
from jax import lax
from jax.experimental import pallas as pl
from jax.experimental.pallas import tpu as pltpu
from jax.sharding import PartitionSpec as P

STOPS = 2
CHUNKS = 2
UP_TILE = 256
DOWN_TILE = 512
NX, NH, NC = 4, 2, 2


def moves():
    def pairs(step):
        made = []
        for x in range(NX):
            for h in range(NH):
                for c in range(NC):
                    x2, h2, c2 = step(x, h, c)
                    made.append((((x * NH) + h) * NC + c, ((x2 % NX) * NH + h2 % NH) * NC + c2 % NC))
        return made

    return {
        "right": pairs(lambda x, h, c: (x + 1, h, c)),
        "left": pairs(lambda x, h, c: (x - 1, h, c)),
        "across": pairs(lambda x, h, c: (x, h + 1, c)),
        "sibling": pairs(lambda x, h, c: (x, h, c + 1)),
    }


MOVES = moves()
PIECES = ((0, 0), (-1, 0), (1, 0), (0, 1), (2, 0), (-1, 1), (1, 1), (2, 1))


def send(value, way):
    return lax.ppermute(value, "expert", MOVES[way])


def next_section(value):
    count = lax.axis_size("section")
    return lax.ppermute(value, "section", [(s, (s + 1) % count) for s in range(count)])


def up_kernel(halves, *refs):
    n = len(PIECES)
    gate_ref, pieces, own_ref, sib_ref, out_ref = refs[0], refs[1 : 1 + n], refs[1 + n], refs[2 + n], refs[3 + n]
    rows_ref, sems = refs[4 + n], refs[5 + n]
    step = pl.program_id(0)
    chunk = pieces[0].shape[0]

    @pl.when(step == 0)
    def _():
        copies = [
            pltpu.make_async_copy(pieces[i], rows_ref.at[pl.ds(i * chunk, chunk)], sems.at[i]) for i in range(n)
        ]
        for copy in copies:
            copy.start()
        for copy in copies:
            copy.wait()

    def emit(w_ref, column):
        acc = jnp.dot(rows_ref[...], w_ref[...], preferred_element_type=jnp.float32)
        out_ref[...] = (acc * jax.nn.sigmoid(acc) * gate_ref[:, column : column + 1]).astype(out_ref.dtype)

    @pl.when(step < halves)
    def _():
        emit(own_ref, 0)

    @pl.when(step >= halves)
    def _():
        emit(sib_ref, 1)


def up_call(gates, pieces, own, sib):
    width, inner = own.shape
    halves = inner // UP_TILE
    rows = sum(p.shape[0] for p in pieces)
    return pl.pallas_call(
        functools.partial(up_kernel, halves),
        grid=(2 * halves,),
        in_specs=[pl.BlockSpec(gates.shape, lambda i: (0, 0))]
        + [pl.BlockSpec(memory_space=pl.ANY)] * len(pieces)
        + [
            pl.BlockSpec((width, UP_TILE), lambda i: (0, jnp.minimum(i, halves - 1))),
            pl.BlockSpec((width, UP_TILE), lambda i: (0, jnp.maximum(i - halves, 0))),
        ],
        out_specs=pl.BlockSpec((rows, UP_TILE), lambda i: (0, i)),
        out_shape=jax.ShapeDtypeStruct((rows, 2 * inner), jnp.bfloat16),
        scratch_shapes=[pltpu.VMEM((rows, width), jnp.bfloat16), pltpu.SemaphoreType.DMA((len(pieces),))],
        compiler_params=pltpu.CompilerParams(vmem_limit_bytes=32 << 20),
        cost_estimate=pl.CostEstimate(
            flops=4 * rows * width * inner,
            bytes_accessed=2 * (rows * width + 2 * width * inner + 2 * rows * inner),
            transcendentals=2 * rows * inner,
        ),
        name="up",
    )(gates, *pieces, own, sib)


def down_kernel(inner, hidden_ref, own_ref, sib_ref, *outs):
    acc = jnp.dot(hidden_ref[:, :inner], own_ref[...], preferred_element_type=jnp.float32)
    acc = acc + jnp.dot(hidden_ref[:, inner:], sib_ref[...], preferred_element_type=jnp.float32)
    chunk = outs[0].shape[0]
    for i, out in enumerate(outs):
        out[...] = acc[i * chunk : (i + 1) * chunk].astype(out.dtype)


def down_call(hidden, own, sib, chunk):
    inner, width = own.shape
    rows = hidden.shape[0]
    count = rows // chunk
    return pl.pallas_call(
        functools.partial(down_kernel, inner),
        grid=(width // DOWN_TILE,),
        in_specs=[
            pl.BlockSpec((rows, 2 * inner), lambda i: (0, 0)),
            pl.BlockSpec((inner, DOWN_TILE), lambda i: (0, i)),
            pl.BlockSpec((inner, DOWN_TILE), lambda i: (0, i)),
        ],
        out_specs=[pl.BlockSpec((chunk, DOWN_TILE), lambda i: (0, i))] * count,
        out_shape=[jax.ShapeDtypeStruct((chunk, width), jnp.bfloat16)] * count,
        compiler_params=pltpu.CompilerParams(vmem_limit_bytes=32 << 20),
        cost_estimate=pl.CostEstimate(
            flops=4 * rows * width * inner,
            bytes_accessed=2 * (rows * width + 2 * width * inner + 2 * rows * inner),
            transcendentals=0,
        ),
        name="down",
    )(hidden, own, sib)


def norm(state, gain_row):
    wide = state.astype(jnp.float32)
    return (wide * lax.rsqrt(jnp.mean(wide * wide, axis=-1, keepdims=True) + 1e-06) * gain_row).astype(jnp.bfloat16)


def spread(own):
    left = send(own, "right")
    right = send(own, "left")
    across = send(own, "across")
    across_right = send(right, "across")
    far = send(left, "right")
    across_left = send(across, "right")
    across_far = send(across_right, "left")
    return own, left, right, across, far, across_left, across_right, across_far


def plus(a, b):
    return (a.astype(jnp.float32) + b.astype(jnp.float32)).astype(jnp.bfloat16)


def gather_back(parts, state):
    own, left, right, across, far, across_left, across_right, across_far = parts
    across_right = plus(across_right, send(across_far, "right"))
    left = plus(left, send(far, "left"))
    across = plus(across, send(across_left, "left"))
    right = plus(right, send(across_right, "across"))
    from_left = send(right, "right")
    from_right = send(left, "left")
    from_across = send(across, "across")
    total = state.astype(jnp.float32) + own.astype(jnp.float32)
    total = total + from_left.astype(jnp.float32) + from_right.astype(jnp.float32) + from_across.astype(jnp.float32)
    return total.astype(jnp.bfloat16)


def body(activations, routes, combine, norm_gain, up_weight, down_weight):
    gain_row = norm_gain[0]
    up_own, down_own = up_weight[0, 0], down_weight[0, 0]
    tokens = activations.shape[1]
    chunk = tokens // CHUNKS
    me = lax.axis_index("expert")
    experts = lax.axis_size("expert")
    core, chip = me % NC, me // NC

    states = [activations[0, c * chunk : (c + 1) * chunk] for c in range(CHUNKS)]
    up_sib = send(up_own, "sibling")
    down_sib = send(down_own, "sibling")

    names = jnp.arange(experts, dtype=jnp.int32)[None, :, None, None]
    dense = jnp.sum(jnp.where(routes[:, 0][:, None] == names, combine[:, 0][:, None], 0.0), axis=-1)
    table = lax.all_gather(dense, "expert", axis=0, tiled=False)
    mine = lax.dynamic_slice_in_dim(table, chip * NC, NC, axis=2)
    mine = jnp.where(core == 0, mine, mine[:, :, ::-1])
    x, h = chip // NH, chip % NH
    sources = [(((x + dx + NX) % NX) * NH + (h + dh) % NH) * NC + core for dx, dh in PIECES]
    mine = jnp.concatenate([lax.dynamic_slice_in_dim(mine, s, 1, axis=0) for s in sources])

    for visit in range(STOPS):
        out = []
        for c in range(CHUNKS):
            gates = mine[:, visit, :, c * chunk : (c + 1) * chunk].transpose(0, 2, 1).reshape(-1, NC)
            pieces = spread(norm(states[c], gain_row))
            hidden = up_call(gates, pieces, up_own, up_sib)
            parts = down_call(hidden, down_own, down_sib, chunk)
            out.append(next_section(gather_back(parts, states[c])))
        states = out
    return jnp.concatenate(states)[None]


def solution(mesh):
    placed = (
        P("section", ("dp", "expert"), None),
        P(None, "section", ("dp", "expert"), None),
        P(None, "section", ("dp", "expert"), None),
        P("section", None),
        P("section", "expert", None, None),
        P("section", "expert", None, None),
    )
    return jax.shard_map(
        body,
        mesh=mesh,
        in_specs=placed,
        out_specs=P("section", ("dp", "expert"), None),
        check_vma=False,
    )
```

```python
import functools

import jax
import jax.numpy as jnp
from jax import lax
from jax.experimental import pallas as pl
from jax.experimental.pallas import tpu as pltpu
from jax.sharding import PartitionSpec as P

STOPS = 2
CHUNKS = 2
UP_TILE = 256
DOWN_TILE = 512
VMEM_LIMIT = 56 << 20
NX, NH, NC = 4, 2, 2


def moves():
    def pairs(step):
        made = []
        for x in range(NX):
            for h in range(NH):
                for c in range(NC):
                    x2, h2, c2 = step(x, h, c)
                    made.append((((x * NH) + h) * NC + c, ((x2 % NX) * NH + h2 % NH) * NC + c2 % NC))
        return made

    return {
        "right": pairs(lambda x, h, c: (x + 1, h, c)),
        "left": pairs(lambda x, h, c: (x - 1, h, c)),
        "across": pairs(lambda x, h, c: (x, h + 1, c)),
        "sibling": pairs(lambda x, h, c: (x, h, c + 1)),
    }


MOVES = moves()


def relative(dx, dh):
    made = []
    for x in range(NX):
        for h in range(NH):
            for c in range(NC):
                made.append(((((x + dx) % NX) * NH + (h + dh) % NH) * NC + c, (x * NH + h) * NC + c))
    return made


PIECES = ((0, 0), (-1, 0), (1, 0), (0, 1), (2, 0), (-1, 1), (1, 1), (2, 1))


def send(value, way):
    return lax.ppermute(value, "expert", MOVES[way])


def next_section(value):
    count = lax.axis_size("section")
    return lax.ppermute(value, "section", [(s, (s + 1) % count) for s in range(count)])


def after(value, *others):
    return lax.optimization_barrier((value,) + others)[0]


def up_kernel(halves, *refs):
    n = (len(refs) - 6)
    gate_ref, pieces, own_ref, sib_ref, out_ref = refs[0], refs[1 : 1 + n], refs[1 + n], refs[2 + n], refs[3 + n]
    rows_ref, sems = refs[4 + n], refs[5 + n]
    step = pl.program_id(0)

    @pl.when(step == 0)
    def _():
        copies, at = [], 0
        for i, piece in enumerate(pieces):
            rows = piece.shape[0]
            copies.append(pltpu.make_async_copy(piece, rows_ref.at[pl.ds(at, rows)], sems.at[i]))
            at += rows
        for copy in copies:
            copy.start()
        for copy in copies:
            copy.wait()

    def emit(w_ref, column):
        acc = jnp.dot(rows_ref[...], w_ref[...], preferred_element_type=jnp.float32)
        out_ref[...] = (acc * jax.nn.sigmoid(acc) * gate_ref[:, column : column + 1]).astype(out_ref.dtype)

    @pl.when(step < halves)
    def _():
        emit(own_ref, 0)

    @pl.when(step >= halves)
    def _():
        emit(sib_ref, 1)


def up_call(gates, pieces, own, sib):
    width, inner = own.shape
    halves = inner // UP_TILE
    rows = sum(p.shape[0] for p in pieces)
    return pl.pallas_call(
        functools.partial(up_kernel, halves),
        grid=(2 * halves,),
        in_specs=[pl.BlockSpec(gates.shape, lambda i: (0, 0))]
        + [pl.BlockSpec(memory_space=pl.ANY)] * len(pieces)
        + [
            pl.BlockSpec((width, UP_TILE), lambda i: (0, jnp.minimum(i, halves - 1))),
            pl.BlockSpec((width, UP_TILE), lambda i: (0, jnp.maximum(i - halves, 0))),
        ],
        out_specs=pl.BlockSpec((rows, UP_TILE), lambda i: (0, i)),
        out_shape=jax.ShapeDtypeStruct((rows, 2 * inner), jnp.bfloat16),
        scratch_shapes=[pltpu.VMEM((rows, width), jnp.bfloat16), pltpu.SemaphoreType.DMA((len(pieces),))],
        compiler_params=pltpu.CompilerParams(vmem_limit_bytes=VMEM_LIMIT),
        cost_estimate=pl.CostEstimate(
            flops=4 * rows * width * inner,
            bytes_accessed=2 * (rows * width + 2 * width * inner + 2 * rows * inner),
            transcendentals=2 * rows * inner,
        ),
        name="up",
    )(gates, *pieces, own, sib)


def down_kernel(inner, hidden_ref, own_ref, sib_ref, *outs):
    acc = jnp.dot(hidden_ref[:, :inner], own_ref[...], preferred_element_type=jnp.float32)
    acc = acc + jnp.dot(hidden_ref[:, inner:], sib_ref[...], preferred_element_type=jnp.float32)
    at = 0
    for out in outs:
        out[...] = acc[at : at + out.shape[0]].astype(out.dtype)
        at += out.shape[0]


def down_call(hidden, own, sib, sizes):
    inner, width = own.shape
    rows = hidden.shape[0]
    return pl.pallas_call(
        functools.partial(down_kernel, inner),
        grid=(width // DOWN_TILE,),
        in_specs=[
            pl.BlockSpec((rows, 2 * inner), lambda i: (0, 0)),
            pl.BlockSpec((inner, DOWN_TILE), lambda i: (0, i)),
            pl.BlockSpec((inner, DOWN_TILE), lambda i: (0, i)),
        ],
        out_specs=[pl.BlockSpec((size, DOWN_TILE), lambda i: (0, i)) for size in sizes],
        out_shape=[jax.ShapeDtypeStruct((size, width), jnp.bfloat16) for size in sizes],
        compiler_params=pltpu.CompilerParams(vmem_limit_bytes=VMEM_LIMIT),
        cost_estimate=pl.CostEstimate(
            flops=4 * rows * width * inner,
            bytes_accessed=2 * (rows * width + 2 * width * inner + 2 * rows * inner),
            transcendentals=0,
        ),
        name="down",
    )(hidden, own, sib)


def norm(state, gain_row):
    wide = state.astype(jnp.float32)
    return (wide * lax.rsqrt(jnp.mean(wide * wide, axis=-1, keepdims=True) + 1e-06) * gain_row).astype(jnp.bfloat16)


def plus(a, b):
    return (a.astype(jnp.float32) + b.astype(jnp.float32)).astype(jnp.bfloat16)


def chunk_rows(sizes):
    starts = [sum(sizes[:i]) for i in range(len(sizes))]
    return [slice(start, start + size) for start, size in zip(starts, sizes)]


def body(activations, routes, combine, norm_gain, up_weight, down_weight):
    gain_row = norm_gain[0]
    up_own, down_own = up_weight[0, 0], down_weight[0, 0]
    tokens = activations.shape[1]
    chunk = tokens // CHUNKS
    spans = chunk_rows([chunk] * CHUNKS)
    me = lax.axis_index("expert")
    experts = lax.axis_size("expert")
    core, chip = me % NC, me // NC

    states = [activations[0, span] for span in spans]
    rows = [norm(state, gain_row) for state in states]
    up_sib = send(up_own, "sibling")
    down_sib = send(down_own, "sibling")

    def gates_of(visit, span):
        return mine[:, visit, :, span].transpose(0, 2, 1).reshape(-1, NC)

    class Chunk:
        pass

    def gather_1(k):
        k.left = send(k.rows, "right")
        k.right = send(k.rows, "left")
        k.across = send(k.rows, "across")

    def gather_2(k):
        k.far_and_left = send(jnp.concatenate([k.left, k.across]), "right")
        k.across_right = send(k.right, "across")

    def gather_3(k):
        k.across_far = send(k.across_right, "left")

    def up(k, *held):
        pieces = [k.rows, k.left, k.right, k.across, k.far_and_left, k.across_right, k.across_far]
        k.hidden = up_call(after(gates_of(k.visit, spans[k.c]), *held), pieces, up_own, up_sib)

    def down(k, *held):
        sizes = [chunk, chunk, chunk, chunk, 2 * chunk, chunk, chunk]
        parts = down_call(after(k.hidden, *held), down_own, down_sib, sizes)
        k.p_own, k.p_left, k.p_right, k.p_across, k.p_far_and_left, k.p_across_right, k.p_across_far = parts

    def return_1(k):
        back = send(k.p_across_far, "right")
        both = send(k.p_far_and_left, "left")
        k.s_across_right = plus(k.p_across_right, back)
        k.s_left = plus(k.p_left, both[:chunk])
        k.s_across = plus(k.p_across, both[chunk:])

    def return_2(k):
        k.s_right = plus(k.p_right, send(k.s_across_right, "across"))

    def return_3(k):
        from_left = send(k.s_right, "right")
        from_right = send(k.s_left, "left")
        from_across = send(k.s_across, "across")
        total = k.state.astype(jnp.float32) + k.p_own.astype(jnp.float32)
        total = total + from_left.astype(jnp.float32) + from_right.astype(jnp.float32) + from_across.astype(jnp.float32)
        k.mixed = total.astype(jnp.bfloat16)

    def onward(k):
        k.next_state = next_section(k.mixed)
        k.next_rows = norm(k.next_state, gain_row)

    def made(c, visit, state, rows):
        k = Chunk()
        k.state, k.rows, k.c, k.visit = state, rows, c, visit
        return k

    a = made(0, 0, states[0], rows[0])
    gather_1(a)
    names = jnp.arange(experts, dtype=jnp.int32)[None, :, None, None]
    dense = jnp.sum(jnp.where(routes[:, 0][:, None] == names, combine[:, 0][:, None], 0.0), axis=-1)
    dense = after(dense, a.left, a.right)
    table = jnp.stack([dense] + [lax.ppermute(dense, "expert", relative(*piece)) for piece in PIECES[1:]])
    mine = lax.dynamic_slice_in_dim(table, chip * NC, NC, axis=2)
    mine = jnp.where(core == 0, mine, mine[:, :, ::-1])

    gather_2(a)
    gather_3(a)
    b = made(1, 0, states[1], after(rows[1], a.across_right))
    gather_1(b)
    up(a)
    down(a, b.left, b.right, b.across)
    for visit in range(STOPS):
        last = visit == STOPS - 1
        return_1(a)
        gather_2(b)
        gather_3(b)
        return_2(a)
        up(b, a.s_across_right)
        return_3(a)
        down(b, a.s_left, a.s_across, a.s_right)
        onward(a)
        return_1(b)
        return_2(b)
        return_3(b)
        onward(b)
        if last:
            return jnp.concatenate([a.next_state, b.next_state])[None]
        c = made(0, visit + 1, a.next_state, a.next_rows)
        gather_1(c)
        gather_2(c)
        gather_3(c)
        d = made(1, visit + 1, b.next_state, b.next_rows)
        gather_1(d)
        up(c, d.rows)
        down(c, d.left, d.right, d.across)
        a, b = c, d


def solution(mesh):
    placed = (
        P("section", ("dp", "expert"), None),
        P(None, "section", ("dp", "expert"), None),
        P(None, "section", ("dp", "expert"), None),
        P("section", None),
        P("section", "expert", None, None),
        P("section", "expert", None, None),
    )
    return jax.shard_map(
        body,
        mesh=mesh,
        in_specs=placed,
        out_specs=P("section", ("dp", "expert"), None),
        check_vma=False,
    )
```

```python
import functools

import jax
import jax.numpy as jnp
from jax import lax
from jax.experimental import pallas as pl
from jax.experimental.pallas import tpu as pltpu
from jax.sharding import PartitionSpec as P

STOPS = 2
CHUNKS = 2
UP_TILE = 256
DOWN_TILE = 512
VMEM_LIMIT = 14 << 20
NX, NH, NC = 4, 2, 2


def moves():
    def pairs(step):
        made = []
        for x in range(NX):
            for h in range(NH):
                for c in range(NC):
                    x2, h2, c2 = step(x, h, c)
                    made.append((((x * NH) + h) * NC + c, ((x2 % NX) * NH + h2 % NH) * NC + c2 % NC))
        return made

    return {
        "right": pairs(lambda x, h, c: (x + 1, h, c)),
        "left": pairs(lambda x, h, c: (x - 1, h, c)),
        "across": pairs(lambda x, h, c: (x, h + 1, c)),
        "sibling": pairs(lambda x, h, c: (x, h, c + 1)),
    }


MOVES = moves()


def send(value, way):
    return lax.ppermute(value, "expert", MOVES[way])


def next_section(value):
    count = lax.axis_size("section")
    return lax.ppermute(value, "section", [(s, (s + 1) % count) for s in range(count)])


def after(value, *others):
    return lax.optimization_barrier((value,) + others)[0]


WHOLE = pl.BlockSpec(memory_space=pltpu.VMEM)
LANES = 128


def params():
    return pltpu.CompilerParams(vmem_limit_bytes=VMEM_LIMIT)


def norm_kernel(visit, span, state_ref, gain_ref, lanes_ref, out_ref):
    width = gain_ref.shape[1]
    wide = state_ref[span, :].astype(jnp.float32)
    scale = lax.rsqrt(jnp.mean(wide * wide, axis=-1, keepdims=True) + 1e-06)
    out_ref[:, :width] = (wide * scale * gain_ref[...]).astype(out_ref.dtype)
    out_ref[:, width:] = lanes_ref[visit, span, :]


def norm_lanes_kernel(visit, span, state_ref, gain_ref, lanes_ref, out_ref):
    width = gain_ref.shape[1]
    wide = state_ref[...].astype(jnp.float32)
    scale = lax.rsqrt(jnp.mean(wide * wide, axis=-1, keepdims=True) + 1e-06)
    out_ref[:, :width] = (wide * scale * gain_ref[...]).astype(out_ref.dtype)
    out_ref[:, width:] = lanes_ref[visit, span, :]


def norm_call(kernel, visit, span, state, gain, lanes):
    rows, width = span.stop - span.start, state.shape[1]
    return pl.pallas_call(
        functools.partial(kernel, visit, span),
        in_specs=[WHOLE] * 3,
        out_specs=WHOLE,
        out_shape=jax.ShapeDtypeStruct((rows, width + LANES), jnp.bfloat16),
        compiler_params=params(),
        cost_estimate=pl.CostEstimate(flops=5 * rows * width, bytes_accessed=4 * rows * width, transcendentals=rows),
        name="norm",
    )(state, gain, lanes)


def up_kernel(n, *refs):
    mask_ref, pieces, weights, out_ref, rows_ref = refs[0], refs[1 : 1 + n], refs[1 + n : 3 + n], refs[3 + n], refs[4 + n]
    width, inner = weights[0].shape
    at, lanes = 0, []
    for piece in pieces:
        rows_ref[at : at + piece.shape[0], :] = piece[:, :width]
        lanes.append(piece[:, width:].astype(jnp.float32))
        at += piece.shape[0]
    lanes = jnp.concatenate(lanes)
    for half, w_ref in enumerate(weights):
        gate = jnp.sum(lanes * mask_ref[half : half + 1, :], axis=-1, keepdims=True)
        for i in range(0, inner, UP_TILE):
            acc = jnp.dot(rows_ref[...], w_ref[:, i : i + UP_TILE], preferred_element_type=jnp.float32)
            out_ref[:, half * inner + i : half * inner + i + UP_TILE] = (acc * jax.nn.sigmoid(acc) * gate).astype(
                out_ref.dtype
            )


def up_call(masks, pieces, own, sib):
    width, inner = own.shape
    rows = sum(p.shape[0] for p in pieces)
    return pl.pallas_call(
        functools.partial(up_kernel, len(pieces)),
        in_specs=[WHOLE] * (len(pieces) + 3),
        out_specs=WHOLE,
        out_shape=jax.ShapeDtypeStruct((rows, 2 * inner), jnp.bfloat16),
        scratch_shapes=[pltpu.VMEM((rows, width), jnp.bfloat16)],
        compiler_params=params(),
        cost_estimate=pl.CostEstimate(
            flops=4 * rows * width * inner,
            bytes_accessed=2 * (rows * width + 2 * width * inner + 2 * rows * inner),
            transcendentals=2 * rows * inner,
        ),
        name="up",
    )(masks, *pieces, own, sib)


def down_kernel(hidden_ref, own_ref, sib_ref, *outs):
    inner, width = own_ref.shape
    for i in range(0, width, DOWN_TILE):
        acc = jnp.dot(hidden_ref[:, :inner], own_ref[:, i : i + DOWN_TILE], preferred_element_type=jnp.float32)
        acc = acc + jnp.dot(hidden_ref[:, inner:], sib_ref[:, i : i + DOWN_TILE], preferred_element_type=jnp.float32)
        at = 0
        for out in outs:
            out[:, i : i + DOWN_TILE] = acc[at : at + out.shape[0]].astype(out.dtype)
            at += out.shape[0]


def down_call(hidden, own, sib, sizes):
    inner, width = own.shape
    rows = hidden.shape[0]
    return pl.pallas_call(
        down_kernel,
        in_specs=[WHOLE] * 3,
        out_specs=[WHOLE] * len(sizes),
        out_shape=[jax.ShapeDtypeStruct((size, width), jnp.bfloat16) for size in sizes],
        compiler_params=params(),
        cost_estimate=pl.CostEstimate(
            flops=4 * rows * width * inner,
            bytes_accessed=2 * (rows * width + 2 * width * inner + 2 * rows * inner),
            transcendentals=0,
        ),
        name="down",
    )(hidden, own, sib)


def plus(a, b):
    return (a.astype(jnp.float32) + b.astype(jnp.float32)).astype(jnp.bfloat16)


def chunk_rows(sizes):
    starts = [sum(sizes[:i]) for i in range(len(sizes))]
    return [slice(start, start + size) for start, size in zip(starts, sizes)]


def body(activations, routes, combine, norm_gain, up_weight, down_weight):
    up_own, down_own = up_weight[0, 0], down_weight[0, 0]
    chunk = activations.shape[1] // CHUNKS
    spans = chunk_rows([chunk] * CHUNKS)
    me = lax.axis_index("expert")
    experts = lax.axis_size("expert")

    lane = jnp.arange(LANES, dtype=jnp.int32)
    dense = jnp.sum(
        jnp.where(routes[:, 0][..., None] == (lane % experts), combine[:, 0][..., None], 0.0), axis=2
    )
    high = lax.reduce_precision(dense, 8, 7)
    lanes = jnp.where(lane < experts, high, jnp.where(lane < 2 * experts, dense - high, 0.0)).astype(jnp.bfloat16)
    served = jnp.stack([me, me + 1 - 2 * (me % NC)])
    masks = ((lane[None, :] % experts == served[:, None]) & (lane[None, :] < 2 * experts)).astype(jnp.float32)

    states = [activations[0, span] for span in spans]
    rows = [norm_call(norm_kernel, 0, span, activations[0], norm_gain, lanes) for span in spans]
    up_sib = send(up_own, "sibling")
    down_sib = send(down_own, "sibling")

    class Chunk:
        pass

    def gather_1(k):
        k.left = send(k.rows, "right")
        k.right = send(k.rows, "left")
        k.across = send(k.rows, "across")

    def gather_2(k):
        k.far_and_left = send(jnp.concatenate([k.left, k.across]), "right")
        k.across_right = send(k.right, "across")

    def gather_3(k):
        k.across_far = send(k.across_right, "left")

    def up(k, *held):
        pieces = [k.rows, k.left, k.right, k.across, k.far_and_left, k.across_right, k.across_far]
        k.hidden = up_call(after(masks, *held), pieces, up_own, up_sib)

    def down(k, *held):
        sizes = [chunk, chunk, chunk, chunk, 2 * chunk, chunk, chunk]
        parts = down_call(after(k.hidden, *held), down_own, down_sib, sizes)
        k.p_own, k.p_left, k.p_right, k.p_across, k.p_far_and_left, k.p_across_right, k.p_across_far = parts

    def return_1(k):
        back = send(k.p_across_far, "right")
        both = send(k.p_far_and_left, "left")
        k.s_across_right = plus(k.p_across_right, back)
        k.s_left = plus(k.p_left, both[:chunk])
        k.s_across = plus(k.p_across, both[chunk:])

    def return_2(k):
        k.s_right = plus(k.p_right, send(k.s_across_right, "across"))

    def return_3(k):
        from_left = send(k.s_right, "right")
        from_right = send(k.s_left, "left")
        from_across = send(k.s_across, "across")
        total = k.state.astype(jnp.float32) + k.p_own.astype(jnp.float32)
        total = total + from_left.astype(jnp.float32) + from_right.astype(jnp.float32) + from_across.astype(jnp.float32)
        k.mixed = total.astype(jnp.bfloat16)

    def onward(k):
        k.next_state = next_section(k.mixed)
        k.next_rows = norm_call(norm_lanes_kernel, k.visit + 1, spans[k.c], k.next_state, norm_gain, lanes)

    def made(c, visit, state, rows):
        k = Chunk()
        k.state, k.rows, k.c, k.visit = state, rows, c, visit
        return k

    a = made(0, 0, states[0], rows[0])
    gather_1(a)
    gather_2(a)
    gather_3(a)
    b = made(1, 0, states[1], after(rows[1], a.across_right))
    gather_1(b)
    up(a)
    down(a, b.left, b.right, b.across)
    for visit in range(STOPS):
        last = visit == STOPS - 1
        return_1(a)
        gather_2(b)
        gather_3(b)
        return_2(a)
        up(b, a.s_across_right)
        return_3(a)
        down(b, a.s_left, a.s_across, a.s_right)
        onward(a)
        return_1(b)
        return_2(b)
        return_3(b)
        onward(b)
        if last:
            return jnp.concatenate([a.next_state, b.next_state])[None]
        c = made(0, visit + 1, a.next_state, a.next_rows)
        gather_1(c)
        gather_2(c)
        gather_3(c)
        d = made(1, visit + 1, b.next_state, b.next_rows)
        gather_1(d)
        up(c, d.rows)
        down(c, d.left, d.right, d.across)
        a, b = c, d


def solution(mesh):
    placed = (
        P("section", ("dp", "expert"), None),
        P(None, "section", ("dp", "expert"), None),
        P(None, "section", ("dp", "expert"), None),
        P("section", None),
        P("section", "expert", None, None),
        P("section", "expert", None, None),
    )
    return jax.shard_map(
        body,
        mesh=mesh,
        in_specs=placed,
        out_specs=P("section", ("dp", "expert"), None),
        check_vma=False,
    )
```

```python
import functools

import jax
import jax.numpy as jnp
from jax import lax
from jax.experimental import pallas as pl
from jax.experimental.pallas import tpu as pltpu
from jax.sharding import PartitionSpec as P

STOPS = 2
CHUNKS = 2
UP_TILE = 256
DOWN_TILE = 512
VMEM_LIMIT = 14 << 20
NX, NH, NC = 4, 2, 2


def moves():
    def pairs(step):
        made = []
        for x in range(NX):
            for h in range(NH):
                for c in range(NC):
                    x2, h2, c2 = step(x, h, c)
                    made.append((((x * NH) + h) * NC + c, ((x2 % NX) * NH + h2 % NH) * NC + c2 % NC))
        return made

    return {
        "right": pairs(lambda x, h, c: (x + 1, h, c)),
        "left": pairs(lambda x, h, c: (x - 1, h, c)),
        "across": pairs(lambda x, h, c: (x, h + 1, c)),
        "sibling": pairs(lambda x, h, c: (x, h, c + 1)),
    }


MOVES = moves()


def send(value, way, k=None, what=""):
    with jax.named_scope(f"{what}_{k.c}_{k.visit}" if k else way):
        return lax.ppermute(value, "expert", MOVES[way])


def next_section(value):
    count = lax.axis_size("section")
    return lax.ppermute(value, "section", [(s, (s + 1) % count) for s in range(count)])


def after(value, *others):
    return lax.optimization_barrier((value,) + others)[0]


WHOLE = pl.BlockSpec(memory_space=pltpu.VMEM)
LANES = 128


def params():
    return pltpu.CompilerParams(vmem_limit_bytes=VMEM_LIMIT)


def norm_kernel(visit, span, state_ref, gain_ref, lanes_ref, out_ref):
    width = gain_ref.shape[1]
    wide = state_ref[span, :].astype(jnp.float32)
    scale = lax.rsqrt(jnp.mean(wide * wide, axis=-1, keepdims=True) + 1e-06)
    out_ref[:, :width] = (wide * scale * gain_ref[...]).astype(out_ref.dtype)
    out_ref[:, width:] = lanes_ref[visit, span, :]


def norm_lanes_kernel(visit, span, state_ref, gain_ref, lanes_ref, out_ref):
    width = gain_ref.shape[1]
    wide = state_ref[...].astype(jnp.float32)
    scale = lax.rsqrt(jnp.mean(wide * wide, axis=-1, keepdims=True) + 1e-06)
    out_ref[:, :width] = (wide * scale * gain_ref[...]).astype(out_ref.dtype)
    out_ref[:, width:] = lanes_ref[visit, span, :]


def norm_call(kernel, visit, span, state, gain, lanes):
    rows, width = span.stop - span.start, state.shape[1]
    return pl.pallas_call(
        functools.partial(kernel, visit, span),
        in_specs=[WHOLE] * 3,
        out_specs=WHOLE,
        out_shape=jax.ShapeDtypeStruct((rows, width + LANES), jnp.bfloat16),
        compiler_params=params(),
        cost_estimate=pl.CostEstimate(flops=5 * rows * width, bytes_accessed=4 * rows * width, transcendentals=rows),
        name="norm",
    )(state, gain, lanes)


def up_kernel(n, *refs):
    mask_ref, pieces, weights, out_ref, rows_ref = refs[0], refs[1 : 1 + n], refs[1 + n : 3 + n], refs[3 + n], refs[4 + n]
    width, inner = weights[0].shape
    at, lanes = 0, []
    for piece in pieces:
        rows_ref[at : at + piece.shape[0], :] = piece[:, :width]
        lanes.append(piece[:, width:].astype(jnp.float32))
        at += piece.shape[0]
    lanes = jnp.concatenate(lanes)
    for half, w_ref in enumerate(weights):
        gate = jnp.sum(lanes * mask_ref[half : half + 1, :], axis=-1, keepdims=True)
        for i in range(0, inner, UP_TILE):
            acc = jnp.dot(rows_ref[...], w_ref[:, i : i + UP_TILE], preferred_element_type=jnp.float32)
            out_ref[:, half * inner + i : half * inner + i + UP_TILE] = (acc * jax.nn.sigmoid(acc) * gate).astype(
                out_ref.dtype
            )


def up_call(masks, pieces, own, sib):
    width, inner = own.shape
    rows = sum(p.shape[0] for p in pieces)
    return pl.pallas_call(
        functools.partial(up_kernel, len(pieces)),
        in_specs=[WHOLE] * (len(pieces) + 3),
        out_specs=WHOLE,
        out_shape=jax.ShapeDtypeStruct((rows, 2 * inner), jnp.bfloat16),
        scratch_shapes=[pltpu.VMEM((rows, width), jnp.bfloat16)],
        compiler_params=params(),
        cost_estimate=pl.CostEstimate(
            flops=4 * rows * width * inner,
            bytes_accessed=2 * (rows * width + 2 * width * inner + 2 * rows * inner),
            transcendentals=2 * rows * inner,
        ),
        name="up",
    )(masks, *pieces, own, sib)


def down_kernel(hidden_ref, own_ref, sib_ref, *outs):
    inner, width = own_ref.shape
    for i in range(0, width, DOWN_TILE):
        acc = jnp.dot(hidden_ref[:, :inner], own_ref[:, i : i + DOWN_TILE], preferred_element_type=jnp.float32)
        acc = acc + jnp.dot(hidden_ref[:, inner:], sib_ref[:, i : i + DOWN_TILE], preferred_element_type=jnp.float32)
        at = 0
        for out in outs:
            out[:, i : i + DOWN_TILE] = acc[at : at + out.shape[0]].astype(out.dtype)
            at += out.shape[0]


def down_call(hidden, own, sib, sizes):
    inner, width = own.shape
    rows = hidden.shape[0]
    return pl.pallas_call(
        down_kernel,
        in_specs=[WHOLE] * 3,
        out_specs=[WHOLE] * len(sizes),
        out_shape=[jax.ShapeDtypeStruct((size, width), jnp.bfloat16) for size in sizes],
        compiler_params=params(),
        cost_estimate=pl.CostEstimate(
            flops=4 * rows * width * inner,
            bytes_accessed=2 * (rows * width + 2 * width * inner + 2 * rows * inner),
            transcendentals=0,
        ),
        name="down",
    )(hidden, own, sib)


def plus_kernel(at, a_ref, b_ref, out_ref):
    other = b_ref[at : at + a_ref.shape[0], :].astype(jnp.float32)
    out_ref[...] = (a_ref[...].astype(jnp.float32) + other).astype(out_ref.dtype)


def plus(a, b, at=0):
    return pl.pallas_call(
        functools.partial(plus_kernel, at),
        in_specs=[WHOLE] * 2,
        out_specs=WHOLE,
        out_shape=jax.ShapeDtypeStruct(a.shape, a.dtype),
        compiler_params=params(),
        cost_estimate=pl.CostEstimate(flops=a.size, bytes_accessed=6 * a.size, transcendentals=0),
        name="plus",
    )(a, b)


def finish_kernel(span, state_ref, *refs):
    total = state_ref[span, :].astype(jnp.float32)
    for ref in refs[:-1]:
        total = total + ref[...].astype(jnp.float32)
    refs[-1][...] = total.astype(refs[-1].dtype)


def finish(state, span, *parts):
    size = parts[0].size
    return pl.pallas_call(
        functools.partial(finish_kernel, span),
        in_specs=[WHOLE] * (1 + len(parts)),
        out_specs=WHOLE,
        out_shape=jax.ShapeDtypeStruct(parts[0].shape, parts[0].dtype),
        compiler_params=params(),
        cost_estimate=pl.CostEstimate(flops=4 * size, bytes_accessed=12 * size, transcendentals=0),
        name="finish",
    )(state, *parts)


def chunk_rows(sizes):
    starts = [sum(sizes[:i]) for i in range(len(sizes))]
    return [slice(start, start + size) for start, size in zip(starts, sizes)]


def body(activations, routes, combine, norm_gain, up_weight, down_weight):
    up_own, down_own = up_weight[0, 0], down_weight[0, 0]
    chunk = activations.shape[1] // CHUNKS
    spans = chunk_rows([chunk] * CHUNKS)
    me = lax.axis_index("expert")
    experts = lax.axis_size("expert")

    lane = jnp.arange(LANES, dtype=jnp.int32)
    dense = jnp.sum(
        jnp.where(routes[:, 0][..., None] == (lane % experts), combine[:, 0][..., None], 0.0), axis=2
    )
    high = lax.reduce_precision(dense, 8, 7)
    lanes = jnp.where(lane < experts, high, jnp.where(lane < 2 * experts, dense - high, 0.0)).astype(jnp.bfloat16)
    served = jnp.stack([me, me + 1 - 2 * (me % NC)])
    masks = ((lane[None, :] % experts == served[:, None]) & (lane[None, :] < 2 * experts)).astype(jnp.float32)

    rows = [norm_call(norm_kernel, 0, span, activations[0], norm_gain, lanes) for span in spans]
    up_sib = send(up_own, "sibling")
    down_sib = send(down_own, "sibling")

    class Chunk:
        pass

    def gather_1(k, held_left=()):
        k.right = send(k.rows, "left", k, "right")
        k.across = send(k.rows, "across", k, "across")
        k.left = send(after(k.rows, *held_left), "right", k, "left")

    def gather_2(k):
        right = after(k.right, *swapped) if k.visit + k.c == 0 else k.right
        k.across_right = send(right, "across", k, "across_right")
        k.pair = jnp.concatenate([k.left, k.across])
        k.far = send(k.pair, "right", k, "far_and_left")

    def gather_3(k):
        k.across_far = send(k.across_right, "left", k, "across_far")

    def up(k, *held):
        pieces = [k.rows, k.left, k.right, k.across, k.far, k.across_right, k.across_far]
        k.hidden = up_call(after(masks, *held), pieces, up_own, up_sib)

    def down(k, *held):
        sizes = [chunk, chunk, chunk, chunk, 2 * chunk, chunk, chunk]
        parts = down_call(after(k.hidden, *held), down_own, down_sib, sizes)
        k.p_own, k.p_left, k.p_right, k.p_across, k.p_far_and_left, k.p_across_right, k.p_across_far = parts

    def return_1(k, held_back=(), held_both=()):
        back = send(after(k.p_across_far, *held_back), "right", k, "back_1_far")
        both = send(after(k.p_far_and_left, *held_both), "left", k, "back_1_both")
        k.s_across_right = plus(k.p_across_right, back)
        k.s_left = plus(k.p_left, both)
        k.s_across = plus(k.p_across, both, chunk)

    def return_2(k):
        k.s_right = plus(k.p_right, send(k.s_across_right, "across", k, "back_2"))

    def return_3(k):
        k.from_left = send(k.s_right, "right", k, "back_3_right")
        k.from_right = send(k.s_left, "left", k, "back_3_left")
        k.from_across = send(k.s_across, "across", k, "back_3_across")
        k.mixed = finish(k.state, k.span, k.p_own, k.from_left, k.from_right, k.from_across)

    def onward(k):
        k.next_state = next_section(k.mixed)
        k.next_rows = norm_call(norm_lanes_kernel, k.visit + 1, spans[k.c], k.next_state, norm_gain, lanes)

    def made(c, visit, state, rows):
        k = Chunk()
        k.state, k.rows, k.c, k.visit = state, rows, c, visit
        k.span = spans[c] if visit == 0 else slice(0, chunk)
        return k

    swapped = (up_sib, down_sib)
    a = made(0, 0, activations[0], rows[0])
    b = made(1, 0, activations[0], rows[1])
    for visit in range(STOPS):
        gather_1(a)
        gather_2(a)
        gather_3(a)
        if visit == 0:
            b.rows = after(b.rows, a.left, a.right, a.across)
        gather_1(b, ())
        gather_2(b)
        gather_3(b)
        up(a, b.right)
        down(a, b.pair, b.across_right)
        return_1(a, (), ())
        return_2(a)
        return_3(a)
        up(b, a.s_across_right)
        down(b, a.s_right)
        return_1(b, (a.mixed,), ())
        return_2(b)
        return_3(b)
        onward(a)
        onward(b)
        if visit == STOPS - 1:
            return jnp.concatenate([a.next_state, b.next_state])[None]
        a, b = made(0, visit + 1, a.next_state, a.next_rows), made(1, visit + 1, b.next_state, b.next_rows)


def solution(mesh):
    placed = (
        P("section", ("dp", "expert"), None),
        P(None, "section", ("dp", "expert"), None),
        P(None, "section", ("dp", "expert"), None),
        P("section", None),
        P("section", "expert", None, None),
        P("section", "expert", None, None),
    )
    return jax.shard_map(
        body,
        mesh=mesh,
        in_specs=placed,
        out_specs=P("section", ("dp", "expert"), None),
        check_vma=False,
    )
```

```python
import functools

import jax
import jax.numpy as jnp
from jax import lax
from jax.experimental import pallas as pl
from jax.experimental.pallas import tpu as pltpu
from jax.sharding import PartitionSpec as P

STOPS = 2
PARTS = (64, 64)
UP_TILE = 256
DOWN_TILE = 512
VMEM_LIMIT = 14 << 20
NX, NH, NC = 4, 2, 2


def moves():
    def pairs(step):
        made = []
        for x in range(NX):
            for h in range(NH):
                for c in range(NC):
                    x2, h2, c2 = step(x, h, c)
                    made.append((((x * NH) + h) * NC + c, ((x2 % NX) * NH + h2 % NH) * NC + c2 % NC))
        return made

    return {
        "right": pairs(lambda x, h, c: (x + 1, h, c)),
        "left": pairs(lambda x, h, c: (x - 1, h, c)),
        "across": pairs(lambda x, h, c: (x, h + 1, c)),
        "sibling": pairs(lambda x, h, c: (x, h, c + 1)),
    }


MOVES = moves()


def send(value, way, k=None, what=""):
    with jax.named_scope(f"{what}_{k.c}_{k.visit}" if k else way):
        return lax.ppermute(value, "expert", MOVES[way])


def next_section(value):
    count = lax.axis_size("section")
    return lax.ppermute(value, "section", [(s, (s + 1) % count) for s in range(count)])


def after(value, *others):
    return lax.optimization_barrier((value,) + others)[0]


WHOLE = pl.BlockSpec(memory_space=pltpu.VMEM)
LANES = 128


def params():
    return pltpu.CompilerParams(vmem_limit_bytes=VMEM_LIMIT)


def norm_kernel(visit, span, state_ref, gain_ref, lanes_ref, out_ref):
    width = gain_ref.shape[1]
    wide = state_ref[span, :].astype(jnp.float32)
    scale = lax.rsqrt(jnp.mean(wide * wide, axis=-1, keepdims=True) + 1e-06)
    out_ref[:, :width] = (wide * scale * gain_ref[...]).astype(out_ref.dtype)
    out_ref[:, width:] = lanes_ref[visit, span, :]


def norm_lanes_kernel(visit, span, state_ref, gain_ref, lanes_ref, out_ref):
    width = gain_ref.shape[1]
    wide = state_ref[...].astype(jnp.float32)
    scale = lax.rsqrt(jnp.mean(wide * wide, axis=-1, keepdims=True) + 1e-06)
    out_ref[:, :width] = (wide * scale * gain_ref[...]).astype(out_ref.dtype)
    out_ref[:, width:] = lanes_ref[visit, span, :]


def norm_call(kernel, visit, span, state, gain, lanes):
    rows, width = span.stop - span.start, state.shape[1]
    return pl.pallas_call(
        functools.partial(kernel, visit, span),
        in_specs=[WHOLE] * 3,
        out_specs=WHOLE,
        out_shape=jax.ShapeDtypeStruct((rows, width + LANES), jnp.bfloat16),
        compiler_params=params(),
        cost_estimate=pl.CostEstimate(flops=5 * rows * width, bytes_accessed=4 * rows * width, transcendentals=rows),
        name="norm",
    )(state, gain, lanes)


def up_kernel(n, *refs):
    mask_ref, pieces, weights, out_ref, rows_ref = refs[0], refs[1 : 1 + n], refs[1 + n : 3 + n], refs[3 + n], refs[4 + n]
    width, inner = weights[0].shape
    at, lanes = 0, []
    for piece in pieces:
        rows_ref[at : at + piece.shape[0], :] = piece[:, :width]
        lanes.append(piece[:, width:].astype(jnp.float32))
        at += piece.shape[0]
    lanes = jnp.concatenate(lanes)
    for half, w_ref in enumerate(weights):
        gate = jnp.sum(lanes * mask_ref[half : half + 1, :], axis=-1, keepdims=True)
        for i in range(0, inner, UP_TILE):
            acc = jnp.dot(rows_ref[...], w_ref[:, i : i + UP_TILE], preferred_element_type=jnp.float32)
            out_ref[:, half * inner + i : half * inner + i + UP_TILE] = (acc * jax.nn.sigmoid(acc) * gate).astype(
                out_ref.dtype
            )


def up_call(masks, pieces, own, sib):
    width, inner = own.shape
    rows = sum(p.shape[0] for p in pieces)
    return pl.pallas_call(
        functools.partial(up_kernel, len(pieces)),
        in_specs=[WHOLE] * (len(pieces) + 3),
        out_specs=WHOLE,
        out_shape=jax.ShapeDtypeStruct((rows, 2 * inner), jnp.bfloat16),
        scratch_shapes=[pltpu.VMEM((rows, width), jnp.bfloat16)],
        compiler_params=params(),
        cost_estimate=pl.CostEstimate(
            flops=4 * rows * width * inner,
            bytes_accessed=2 * (rows * width + 2 * width * inner + 2 * rows * inner),
            transcendentals=2 * rows * inner,
        ),
        name="up",
    )(masks, *pieces, own, sib)


def down_kernel(hidden_ref, own_ref, sib_ref, *outs):
    inner, width = own_ref.shape
    for i in range(0, width, DOWN_TILE):
        acc = jnp.dot(hidden_ref[:, :inner], own_ref[:, i : i + DOWN_TILE], preferred_element_type=jnp.float32)
        acc = acc + jnp.dot(hidden_ref[:, inner:], sib_ref[:, i : i + DOWN_TILE], preferred_element_type=jnp.float32)
        at = 0
        for out in outs:
            out[:, i : i + DOWN_TILE] = acc[at : at + out.shape[0]].astype(out.dtype)
            at += out.shape[0]


def down_call(hidden, own, sib, sizes):
    inner, width = own.shape
    rows = hidden.shape[0]
    return pl.pallas_call(
        down_kernel,
        in_specs=[WHOLE] * 3,
        out_specs=[WHOLE] * len(sizes),
        out_shape=[jax.ShapeDtypeStruct((size, width), jnp.bfloat16) for size in sizes],
        compiler_params=params(),
        cost_estimate=pl.CostEstimate(
            flops=4 * rows * width * inner,
            bytes_accessed=2 * (rows * width + 2 * width * inner + 2 * rows * inner),
            transcendentals=0,
        ),
        name="down",
    )(hidden, own, sib)


def plus_kernel(at, a_ref, b_ref, out_ref):
    other = b_ref[at : at + a_ref.shape[0], :].astype(jnp.float32)
    out_ref[...] = (a_ref[...].astype(jnp.float32) + other).astype(out_ref.dtype)


def plus(a, b, at=0):
    return pl.pallas_call(
        functools.partial(plus_kernel, at),
        in_specs=[WHOLE] * 2,
        out_specs=WHOLE,
        out_shape=jax.ShapeDtypeStruct(a.shape, a.dtype),
        compiler_params=params(),
        cost_estimate=pl.CostEstimate(flops=a.size, bytes_accessed=6 * a.size, transcendentals=0),
        name="plus",
    )(a, b)


def finish_kernel(span, state_ref, *refs):
    total = state_ref[span, :].astype(jnp.float32)
    for ref in refs[:-1]:
        total = total + ref[...].astype(jnp.float32)
    refs[-1][...] = total.astype(refs[-1].dtype)


def finish(state, span, *parts):
    size = parts[0].size
    return pl.pallas_call(
        functools.partial(finish_kernel, span),
        in_specs=[WHOLE] * (1 + len(parts)),
        out_specs=WHOLE,
        out_shape=jax.ShapeDtypeStruct(parts[0].shape, parts[0].dtype),
        compiler_params=params(),
        cost_estimate=pl.CostEstimate(flops=4 * size, bytes_accessed=12 * size, transcendentals=0),
        name="finish",
    )(state, *parts)


def chunk_rows(sizes):
    starts = [sum(sizes[:i]) for i in range(len(sizes))]
    return [slice(start, start + size) for start, size in zip(starts, sizes)]


def body(activations, routes, combine, norm_gain, up_weight, down_weight):
    up_own, down_own = up_weight[0, 0], down_weight[0, 0]
    sizes_of = [activations.shape[1] * part // 128 for part in PARTS]
    spans = chunk_rows(sizes_of)
    me = lax.axis_index("expert")
    experts = lax.axis_size("expert")

    lane = jnp.arange(LANES, dtype=jnp.int32)
    dense = jnp.sum(
        jnp.where(routes[:, 0][..., None] == (lane % experts), combine[:, 0][..., None], 0.0), axis=2
    )
    high = lax.reduce_precision(dense, 8, 7)
    lanes = jnp.where(lane < experts, high, jnp.where(lane < 2 * experts, dense - high, 0.0)).astype(jnp.bfloat16)
    served = jnp.stack([me, me + 1 - 2 * (me % NC)])
    masks = ((lane[None, :] % experts == served[:, None]) & (lane[None, :] < 2 * experts)).astype(jnp.float32)

    rows = [norm_call(norm_kernel, 0, span, activations[0], norm_gain, lanes) for span in spans]
    up_sib = send(up_own, "sibling")
    down_sib = send(down_own, "sibling")

    class Chunk:
        pass

    def gather_1(k, held_right=(), held_across=(), held_left=()):
        k.right = send(after(k.rows, *held_right), "left", k, "right")
        k.across = send(after(k.rows, *held_across), "across", k, "across")
        k.left = send(after(k.rows, *held_left), "right", k, "left")

    def gather_2(k):
        ready = swapped if k.visit + k.c == 7 else ()
        k.across_right = send(after(k.right, *ready), "across", k, "across_right")
        k.pair = jnp.concatenate([after(k.left, *ready), k.across])
        k.far = send(k.pair, "right", k, "far_and_left")

    def gather_3(k):
        k.across_far = send(k.across_right, "left", k, "across_far")

    def up(k, *held):
        pieces = [k.rows, k.left, k.right, k.across, k.far, k.across_right, k.across_far]
        k.hidden = up_call(after(masks, *held), pieces, up_own, up_sib)

    def down(k, *held):
        sizes = [k.size] * 4 + [2 * k.size] + [k.size] * 2
        parts = down_call(after(k.hidden, *held), down_own, down_sib, sizes)
        k.p_own, k.p_left, k.p_right, k.p_across, k.p_far_and_left, k.p_across_right, k.p_across_far = parts

    def return_1(k, held_back=(), held_both=()):
        back = send(after(k.p_across_far, *held_back), "right", k, "back_1_far")
        both = send(after(k.p_far_and_left, *held_both), "left", k, "back_1_both")
        k.s_across_right = plus(k.p_across_right, back)
        k.s_left = plus(k.p_left, both)
        k.s_across = plus(k.p_across, both, k.size)

    def return_2(k):
        k.s_right = plus(k.p_right, send(k.s_across_right, "across", k, "back_2"))

    def return_3(k, held=()):
        k.from_left = send(after(k.s_right, *held), "right", k, "back_3_right")
        k.from_right = send(after(k.s_left, *held), "left", k, "back_3_left")
        k.from_across = send(after(k.s_across, *held), "across", k, "back_3_across")
        k.mixed = finish(k.state, k.span, k.p_own, k.from_left, k.from_right, k.from_across)

    def onward(k):
        k.next_state = next_section(k.mixed)
        k.next_rows = norm_call(norm_lanes_kernel, k.visit + 1, spans[k.c], k.next_state, norm_gain, lanes)

    def made(c, visit, state, rows):
        k = Chunk()
        k.state, k.rows, k.c, k.visit = state, rows, c, visit
        k.size = sizes_of[c]
        k.span = spans[c] if visit == 0 else slice(0, k.size)
        return k

    swapped = (up_sib, down_sib)
    a = made(0, 0, activations[0], rows[0])
    b = made(1, 0, activations[0], rows[1])
    for visit in range(STOPS):
        first = visit == 0
        swap = (up_sib, down_sib,) if first else ()
        gather_1(a)
        gather_2(a)
        gather_3(a)
        gather_1(b, ((a.left, a.right, a.across,) if first else (a.across_right,)) + swap, ((a.across_right,) if first else (a.across_right,)) + swap, ((a.far,) if first else ()) + swap)
        gather_2(b)
        gather_3(b)
        up(a, b.right)
        down(a, b.pair, b.across_right)
        return_1(a, (), ())
        return_2(a)
        return_3(a)
        onward(a)
        up(b)
        down(b, a.s_left, a.s_across)
        return_1(b, (), ())
        return_2(b)
        return_3(b, ())
        onward(b)
        if visit == STOPS - 1:
            return jnp.concatenate([a.next_state, b.next_state])[None]
        a, b = made(0, visit + 1, a.next_state, a.next_rows), made(1, visit + 1, b.next_state, b.next_rows)


def solution(mesh):
    placed = (
        P("section", ("dp", "expert"), None),
        P(None, "section", ("dp", "expert"), None),
        P(None, "section", ("dp", "expert"), None),
        P("section", None),
        P("section", "expert", None, None),
        P("section", "expert", None, None),
    )
    return jax.shard_map(
        body,
        mesh=mesh,
        in_specs=placed,
        out_specs=P("section", ("dp", "expert"), None),
        check_vma=False,
    )
```

```python
import functools

import jax
import jax.numpy as jnp
from jax import lax
from jax.experimental import pallas as pl
from jax.experimental.pallas import tpu as pltpu
from jax.sharding import PartitionSpec as P

STOPS = 2
PARTS = (64, 64)
UP_TILE = 256
DOWN_TILE = 512
VMEM_LIMIT = 14 << 20
NX, NH, NC = 4, 2, 2


def moves():
    def pairs(step):
        made = []
        for x in range(NX):
            for h in range(NH):
                for c in range(NC):
                    x2, h2, c2 = step(x, h, c)
                    made.append((((x * NH) + h) * NC + c, ((x2 % NX) * NH + h2 % NH) * NC + c2 % NC))
        return made

    return {
        "right": pairs(lambda x, h, c: (x + 1, h, c)),
        "left": pairs(lambda x, h, c: (x - 1, h, c)),
        "across": pairs(lambda x, h, c: (x, h + 1, c)),
        "sibling": pairs(lambda x, h, c: (x, h, c + 1)),
    }


MOVES = moves()


def send(value, way, k=None, what=""):
    with jax.named_scope(f"{what}_{k.c}_{k.visit}" if k else way):
        return lax.ppermute(value, "expert", MOVES[way])


def next_section(value):
    count = lax.axis_size("section")
    return lax.ppermute(value, "section", [(s, (s + 1) % count) for s in range(count)])


def after(value, *others):
    return lax.optimization_barrier((value,) + others)[0]


WHOLE = pl.BlockSpec(memory_space=pltpu.VMEM)
LANES = 128


def params():
    return pltpu.CompilerParams(vmem_limit_bytes=VMEM_LIMIT)


def norm_kernel(visit, span, state_ref, gain_ref, lanes_ref, out_ref):
    width = gain_ref.shape[1]
    wide = state_ref[span, :].astype(jnp.float32)
    scale = lax.rsqrt(jnp.mean(wide * wide, axis=-1, keepdims=True) + 1e-06)
    out_ref[:, :width] = (wide * scale * gain_ref[...]).astype(out_ref.dtype)
    out_ref[:, width:] = lanes_ref[visit, span, :]


def norm_lanes_kernel(visit, span, state_ref, gain_ref, lanes_ref, out_ref):
    width = gain_ref.shape[1]
    wide = state_ref[...].astype(jnp.float32)
    scale = lax.rsqrt(jnp.mean(wide * wide, axis=-1, keepdims=True) + 1e-06)
    out_ref[:, :width] = (wide * scale * gain_ref[...]).astype(out_ref.dtype)
    out_ref[:, width:] = lanes_ref[visit, span, :]


def norm_call(kernel, visit, span, state, gain, lanes):
    rows, width = span.stop - span.start, state.shape[1]
    return pl.pallas_call(
        functools.partial(kernel, visit, span),
        in_specs=[WHOLE] * 3,
        out_specs=WHOLE,
        out_shape=jax.ShapeDtypeStruct((rows, width + LANES), jnp.bfloat16),
        compiler_params=params(),
        cost_estimate=pl.CostEstimate(flops=5 * rows * width, bytes_accessed=4 * rows * width, transcendentals=rows),
        name="norm",
    )(state, gain, lanes)


def up_kernel(n, *refs):
    mask_ref, pieces, weights, out_ref, rows_ref = refs[0], refs[1 : 1 + n], refs[1 + n : 3 + n], refs[3 + n], refs[4 + n]
    width, inner = weights[0].shape
    at, lanes = 0, []
    for piece in pieces:
        rows_ref[at : at + piece.shape[0], :] = piece[:, :width]
        lanes.append(piece[:, width:].astype(jnp.float32))
        at += piece.shape[0]
    lanes = jnp.concatenate(lanes)
    for half, w_ref in enumerate(weights):
        gate = jnp.sum(lanes * mask_ref[half : half + 1, :], axis=-1, keepdims=True)
        for i in range(0, inner, UP_TILE):
            acc = jnp.dot(rows_ref[...], w_ref[:, i : i + UP_TILE], preferred_element_type=jnp.float32)
            out_ref[:, half * inner + i : half * inner + i + UP_TILE] = (acc * jax.nn.sigmoid(acc) * gate).astype(
                out_ref.dtype
            )


def up_call(masks, pieces, own, sib):
    width, inner = own.shape
    rows = sum(p.shape[0] for p in pieces)
    return pl.pallas_call(
        functools.partial(up_kernel, len(pieces)),
        in_specs=[WHOLE] * (len(pieces) + 3),
        out_specs=WHOLE,
        out_shape=jax.ShapeDtypeStruct((rows, 2 * inner), jnp.bfloat16),
        scratch_shapes=[pltpu.VMEM((rows, width), jnp.bfloat16)],
        compiler_params=params(),
        cost_estimate=pl.CostEstimate(
            flops=4 * rows * width * inner,
            bytes_accessed=2 * (rows * width + 2 * width * inner + 2 * rows * inner),
            transcendentals=2 * rows * inner,
        ),
        name="up",
    )(masks, *pieces, own, sib)


def down_kernel(hidden_ref, own_ref, sib_ref, *outs):
    inner, width = own_ref.shape
    for i in range(0, width, DOWN_TILE):
        acc = jnp.dot(hidden_ref[:, :inner], own_ref[:, i : i + DOWN_TILE], preferred_element_type=jnp.float32)
        acc = acc + jnp.dot(hidden_ref[:, inner:], sib_ref[:, i : i + DOWN_TILE], preferred_element_type=jnp.float32)
        at = 0
        for out in outs:
            out[:, i : i + DOWN_TILE] = acc[at : at + out.shape[0]].astype(out.dtype)
            at += out.shape[0]


def down_call(hidden, own, sib, sizes):
    inner, width = own.shape
    rows = hidden.shape[0]
    return pl.pallas_call(
        down_kernel,
        in_specs=[WHOLE] * 3,
        out_specs=[WHOLE] * len(sizes),
        out_shape=[jax.ShapeDtypeStruct((size, width), jnp.bfloat16) for size in sizes],
        compiler_params=params(),
        cost_estimate=pl.CostEstimate(
            flops=4 * rows * width * inner,
            bytes_accessed=2 * (rows * width + 2 * width * inner + 2 * rows * inner),
            transcendentals=0,
        ),
        name="down",
    )(hidden, own, sib)


def plus_kernel(at, a_ref, b_ref, out_ref):
    other = b_ref[at : at + a_ref.shape[0], :].astype(jnp.float32)
    out_ref[...] = (a_ref[...].astype(jnp.float32) + other).astype(out_ref.dtype)


def plus(a, b, at=0):
    return pl.pallas_call(
        functools.partial(plus_kernel, at),
        in_specs=[WHOLE] * 2,
        out_specs=WHOLE,
        out_shape=jax.ShapeDtypeStruct(a.shape, a.dtype),
        compiler_params=params(),
        cost_estimate=pl.CostEstimate(flops=a.size, bytes_accessed=6 * a.size, transcendentals=0),
        name="plus",
    )(a, b)


def finish_kernel(span, state_ref, *refs):
    total = state_ref[span, :].astype(jnp.float32)
    for ref in refs[:-1]:
        total = total + ref[...].astype(jnp.float32)
    refs[-1][...] = total.astype(refs[-1].dtype)


def finish(state, span, *parts):
    size = parts[0].size
    return pl.pallas_call(
        functools.partial(finish_kernel, span),
        in_specs=[WHOLE] * (1 + len(parts)),
        out_specs=WHOLE,
        out_shape=jax.ShapeDtypeStruct(parts[0].shape, parts[0].dtype),
        compiler_params=params(),
        cost_estimate=pl.CostEstimate(flops=4 * size, bytes_accessed=12 * size, transcendentals=0),
        name="finish",
    )(state, *parts)


def chunk_rows(sizes):
    starts = [sum(sizes[:i]) for i in range(len(sizes))]
    return [slice(start, start + size) for start, size in zip(starts, sizes)]


def body(activations, routes, combine, norm_gain, up_weight, down_weight):
    up_own, down_own = up_weight[0, 0], down_weight[0, 0]
    sizes_of = [activations.shape[1] * part // 128 for part in PARTS]
    spans = chunk_rows(sizes_of)
    me = lax.axis_index("expert")
    experts = lax.axis_size("expert")

    lane = jnp.arange(LANES, dtype=jnp.int32)
    dense = jnp.sum(
        jnp.where(routes[:, 0][..., None] == (lane % experts), combine[:, 0][..., None], 0.0), axis=2
    )
    high = lax.reduce_precision(dense, 8, 7)
    lanes = jnp.where(lane < experts, high, jnp.where(lane < 2 * experts, dense - high, 0.0)).astype(jnp.bfloat16)
    served = jnp.stack([me, me + 1 - 2 * (me % NC)])
    masks = ((lane[None, :] % experts == served[:, None]) & (lane[None, :] < 2 * experts)).astype(jnp.float32)

    rows = [norm_call(norm_kernel, 0, span, activations[0], norm_gain, lanes) for span in spans]
    up_sib = send(up_own, "sibling")
    down_sib = send(down_own, "sibling")

    class Chunk:
        pass

    def gather_1(k, held_right=(), held_across=(), held_left=()):
        k.right = send(after(k.rows, *held_right), "left", k, "right")
        k.across = send(after(k.rows, *held_across), "across", k, "across")
        k.left = send(after(k.rows, *held_left), "right", k, "left")

    def gather_2(k):
        ready = swapped if k.visit + k.c == 7 else ()
        k.across_right = send(after(k.right, *ready), "across", k, "across_right")
        k.pair = jnp.concatenate([after(k.left, *ready), k.across])
        k.far = send(k.pair, "right", k, "far_and_left")

    def gather_3(k):
        k.across_far = send(k.across_right, "left", k, "across_far")

    def up(k, *held):
        pieces = [k.rows, k.left, k.right, k.across, k.far, k.across_right, k.across_far]
        k.hidden = up_call(after(masks, *held), pieces, up_own, up_sib)

    def down(k, *held):
        sizes = [k.size] * 4 + [2 * k.size] + [k.size] * 2
        parts = down_call(after(k.hidden, *held), down_own, down_sib, sizes)
        k.p_own, k.p_left, k.p_right, k.p_across, k.p_far_and_left, k.p_across_right, k.p_across_far = parts

    def return_1(k, held_back=(), held_both=()):
        back = send(after(k.p_across_far, *held_back), "right", k, "back_1_far")
        both = send(after(k.p_far_and_left, *held_both), "left", k, "back_1_both")
        k.s_across_right = plus(k.p_across_right, back)
        k.s_left = plus(k.p_left, both)
        k.s_across = plus(k.p_across, both, k.size)

    def return_2(k):
        k.s_right = plus(k.p_right, send(k.s_across_right, "across", k, "back_2"))

    def return_3(k, held_right=(), held_left=(), held_across=()):
        k.from_left = send(after(k.s_right, *held_right), "right", k, "back_3_right")
        k.from_right = send(after(k.s_left, *held_left), "left", k, "back_3_left")
        k.from_across = send(after(k.s_across, *held_across), "across", k, "back_3_across")
        k.mixed = finish(k.state, k.span, k.p_own, k.from_left, k.from_right, k.from_across)

    def onward(k, held=()):
        k.next_state = next_section(k.mixed)
        ready = after(k.next_state, *held)
        k.next_rows = norm_call(norm_lanes_kernel, k.visit + 1, spans[k.c], ready, norm_gain, lanes)

    def made(c, visit, state, rows):
        k = Chunk()
        k.state, k.rows, k.c, k.visit = state, rows, c, visit
        k.size = sizes_of[c]
        k.span = spans[c] if visit == 0 else slice(0, k.size)
        return k

    swapped = (up_sib, down_sib)
    a = made(0, 0, activations[0], rows[0])
    b = made(1, 0, activations[0], rows[1])
    for visit in range(STOPS):
        first = visit == 0
        if first:
            gather_1(a)
            gather_2(a)
            gather_3(a)
        swap = (up_sib, down_sib,) if first else ()
        gather_1(b, ((a.left, a.right, a.across,) if first else (a.across_right,)) + swap, ((a.across_right,) if first else (a.across_right,)) + swap, ((a.far,) if first else ()) + swap)
        gather_2(b)
        gather_3(b)
        up(a, *((b.right,) if first else (b.right,)))
        down(a, *((b.pair, b.across_right,) if first else (b.pair, b.across_right,)))
        return_1(a, (b.far,), ())
        return_2(a)
        return_3(a)
        onward(a)
        up(b, *(() if first else ()))
        down(b, *((a.s_left, a.s_across,) if first else (a.s_across_right,)))
        return_1(b, () if first else (a.s_right,), () if first else ())
        return_2(b)
        if visit == STOPS - 1:
            return_3(b)
            onward(b)
            return jnp.concatenate([a.next_state, b.next_state])[None]
        c = made(0, visit + 1, a.next_state, a.next_rows)
        gather_1(c)
        gather_2(c)
        gather_3(c)
        return_3(b, (), (), ())
        onward(b, ())
        a, b = c, made(1, visit + 1, b.next_state, b.next_rows)


def solution(mesh):
    placed = (
        P("section", ("dp", "expert"), None),
        P(None, "section", ("dp", "expert"), None),
        P(None, "section", ("dp", "expert"), None),
        P("section", None),
        P("section", "expert", None, None),
        P("section", "expert", None, None),
    )
    return jax.shard_map(
        body,
        mesh=mesh,
        in_specs=placed,
        out_specs=P("section", ("dp", "expert"), None),
        check_vma=False,
    )
```

```python
import functools

import jax
import jax.numpy as jnp
from jax import lax
from jax.experimental import pallas as pl
from jax.experimental.pallas import tpu as pltpu
from jax.sharding import PartitionSpec as P

STOPS = 2
PARTS = (64, 64)
UP_TILE = 256
DOWN_TILE = 512
VMEM_LIMIT = 14 << 20
NX, NH, NC = 4, 2, 2


def moves():
    def pairs(step):
        made = []
        for x in range(NX):
            for h in range(NH):
                for c in range(NC):
                    x2, h2, c2 = step(x, h, c)
                    made.append((((x * NH) + h) * NC + c, ((x2 % NX) * NH + h2 % NH) * NC + c2 % NC))
        return made

    return {
        "right": pairs(lambda x, h, c: (x + 1, h, c)),
        "left": pairs(lambda x, h, c: (x - 1, h, c)),
        "across": pairs(lambda x, h, c: (x, h + 1, c)),
        "sibling": pairs(lambda x, h, c: (x, h, c + 1)),
    }


MOVES = moves()


def send(value, way, k=None, what=""):
    with jax.named_scope(f"{what}_{k.c}_{k.visit}" if k else way):
        return lax.ppermute(value, "expert", MOVES[way])


def next_section(value):
    count = lax.axis_size("section")
    return lax.ppermute(value, "section", [(s, (s + 1) % count) for s in range(count)])


def after(value, *others):
    return lax.optimization_barrier((value,) + others)[0]


WHOLE = pl.BlockSpec(memory_space=pltpu.VMEM)
LANES = 128


def params():
    return pltpu.CompilerParams(vmem_limit_bytes=VMEM_LIMIT)


def norm_kernel(visit, span, state_ref, gain_ref, lanes_ref, out_ref):
    width = gain_ref.shape[1]
    wide = state_ref[span, :].astype(jnp.float32)
    scale = lax.rsqrt(jnp.mean(wide * wide, axis=-1, keepdims=True) + 1e-06)
    out_ref[:, :width] = (wide * scale * gain_ref[...]).astype(out_ref.dtype)
    out_ref[:, width:] = lanes_ref[visit, span, :]


def norm_lanes_kernel(visit, span, state_ref, gain_ref, lanes_ref, out_ref):
    width = gain_ref.shape[1]
    wide = state_ref[...].astype(jnp.float32)
    scale = lax.rsqrt(jnp.mean(wide * wide, axis=-1, keepdims=True) + 1e-06)
    out_ref[:, :width] = (wide * scale * gain_ref[...]).astype(out_ref.dtype)
    out_ref[:, width:] = lanes_ref[visit, span, :]


def norm_call(kernel, visit, span, state, gain, lanes):
    rows, width = span.stop - span.start, state.shape[1]
    return pl.pallas_call(
        functools.partial(kernel, visit, span),
        in_specs=[WHOLE] * 3,
        out_specs=WHOLE,
        out_shape=jax.ShapeDtypeStruct((rows, width + LANES), jnp.bfloat16),
        compiler_params=params(),
        cost_estimate=pl.CostEstimate(flops=5 * rows * width, bytes_accessed=4 * rows * width, transcendentals=rows),
        name="norm",
    )(state, gain, lanes)


def up_kernel(n, *refs):
    mask_ref, pieces, weights, out_ref, rows_ref = refs[0], refs[1 : 1 + n], refs[1 + n : 3 + n], refs[3 + n], refs[4 + n]
    width, inner = weights[0].shape
    at, lanes = 0, []
    for piece in pieces:
        rows_ref[at : at + piece.shape[0], :] = piece[:, :width]
        lanes.append(piece[:, width:].astype(jnp.float32))
        at += piece.shape[0]
    lanes = jnp.concatenate(lanes)
    for half, w_ref in enumerate(weights):
        gate = jnp.sum(lanes * mask_ref[half : half + 1, :], axis=-1, keepdims=True)
        for i in range(0, inner, UP_TILE):
            acc = jnp.dot(rows_ref[...], w_ref[:, i : i + UP_TILE], preferred_element_type=jnp.float32)
            out_ref[:, half * inner + i : half * inner + i + UP_TILE] = (acc * jax.nn.sigmoid(acc) * gate).astype(
                out_ref.dtype
            )


def up_call(masks, pieces, own, sib):
    width, inner = own.shape
    rows = sum(p.shape[0] for p in pieces)
    return pl.pallas_call(
        functools.partial(up_kernel, len(pieces)),
        in_specs=[WHOLE] * (len(pieces) + 3),
        out_specs=WHOLE,
        out_shape=jax.ShapeDtypeStruct((rows, 2 * inner), jnp.bfloat16),
        scratch_shapes=[pltpu.VMEM((rows, width), jnp.bfloat16)],
        compiler_params=params(),
        cost_estimate=pl.CostEstimate(
            flops=4 * rows * width * inner,
            bytes_accessed=2 * (rows * width + 2 * width * inner + 2 * rows * inner),
            transcendentals=2 * rows * inner,
        ),
        name="up",
    )(masks, *pieces, own, sib)


def down_kernel(hidden_ref, own_ref, sib_ref, *outs):
    inner, width = own_ref.shape
    for i in range(0, width, DOWN_TILE):
        acc = jnp.dot(hidden_ref[:, :inner], own_ref[:, i : i + DOWN_TILE], preferred_element_type=jnp.float32)
        acc = acc + jnp.dot(hidden_ref[:, inner:], sib_ref[:, i : i + DOWN_TILE], preferred_element_type=jnp.float32)
        at = 0
        for out in outs:
            out[:, i : i + DOWN_TILE] = acc[at : at + out.shape[0]].astype(out.dtype)
            at += out.shape[0]


def down_call(hidden, own, sib, sizes):
    inner, width = own.shape
    rows = hidden.shape[0]
    return pl.pallas_call(
        down_kernel,
        in_specs=[WHOLE] * 3,
        out_specs=[WHOLE] * len(sizes),
        out_shape=[jax.ShapeDtypeStruct((size, width), jnp.bfloat16) for size in sizes],
        compiler_params=params(),
        cost_estimate=pl.CostEstimate(
            flops=4 * rows * width * inner,
            bytes_accessed=2 * (rows * width + 2 * width * inner + 2 * rows * inner),
            transcendentals=0,
        ),
        name="down",
    )(hidden, own, sib)


def plus_kernel(at, a_ref, b_ref, out_ref):
    other = b_ref[at : at + a_ref.shape[0], :].astype(jnp.float32)
    out_ref[...] = (a_ref[...].astype(jnp.float32) + other).astype(out_ref.dtype)


def plus(a, b, at=0):
    return pl.pallas_call(
        functools.partial(plus_kernel, at),
        in_specs=[WHOLE] * 2,
        out_specs=WHOLE,
        out_shape=jax.ShapeDtypeStruct(a.shape, a.dtype),
        compiler_params=params(),
        cost_estimate=pl.CostEstimate(flops=a.size, bytes_accessed=6 * a.size, transcendentals=0),
        name="plus",
    )(a, b)


def finish_kernel(span, state_ref, *refs):
    total = state_ref[span, :].astype(jnp.float32)
    for ref in refs[:-1]:
        total = total + ref[...].astype(jnp.float32)
    refs[-1][...] = total.astype(refs[-1].dtype)


def finish(state, span, *parts):
    size = parts[0].size
    return pl.pallas_call(
        functools.partial(finish_kernel, span),
        in_specs=[WHOLE] * (1 + len(parts)),
        out_specs=WHOLE,
        out_shape=jax.ShapeDtypeStruct(parts[0].shape, parts[0].dtype),
        compiler_params=params(),
        cost_estimate=pl.CostEstimate(flops=4 * size, bytes_accessed=12 * size, transcendentals=0),
        name="finish",
    )(state, *parts)


def chunk_rows(sizes):
    starts = [sum(sizes[:i]) for i in range(len(sizes))]
    return [slice(start, start + size) for start, size in zip(starts, sizes)]


def body(activations, routes, combine, norm_gain, up_weight, down_weight):
    up_own, down_own = up_weight[0, 0], down_weight[0, 0]
    sizes_of = [activations.shape[1] * part // 128 for part in PARTS]
    spans = chunk_rows(sizes_of)
    me = lax.axis_index("expert")
    experts = lax.axis_size("expert")

    lane = jnp.arange(LANES, dtype=jnp.int32)
    dense = jnp.sum(
        jnp.where(routes[:, 0][..., None] == (lane % experts), combine[:, 0][..., None], 0.0), axis=2
    )
    high = lax.reduce_precision(dense, 8, 7)
    lanes = jnp.where(lane < experts, high, jnp.where(lane < 2 * experts, dense - high, 0.0)).astype(jnp.bfloat16)
    served = jnp.stack([me, me + 1 - 2 * (me % NC)])
    masks = ((lane[None, :] % experts == served[:, None]) & (lane[None, :] < 2 * experts)).astype(jnp.float32)

    rows = [norm_call(norm_kernel, 0, span, activations[0], norm_gain, lanes) for span in spans]
    up_sib = send(up_own, "sibling")
    down_sib = send(down_own, "sibling")

    class Chunk:
        pass

    def gather_1(k, held_right=(), held_across=(), held_left=()):
        k.right = send(after(k.rows, *held_right), "left", k, "right")
        k.across = send(after(k.rows, *held_across), "across", k, "across")
        k.left = send(after(k.rows, *held_left), "right", k, "left")

    def gather_2(k):
        ready = swapped if k.visit + k.c == 7 else ()
        k.across_right = send(after(k.right, *ready), "across", k, "across_right")
        k.pair = jnp.concatenate([after(k.left, *ready), k.across])
        k.far = send(k.pair, "right", k, "far_and_left")

    def gather_3(k):
        k.across_far = send(k.across_right, "left", k, "across_far")

    def up(k, *held):
        pieces = [k.rows, k.left, k.right, k.across, k.far, k.across_right, k.across_far]
        k.hidden = up_call(after(masks, *held), pieces, up_own, up_sib)

    def down(k, *held):
        sizes = [k.size] * 4 + [2 * k.size] + [k.size] * 2
        parts = down_call(after(k.hidden, *held), down_own, down_sib, sizes)
        k.p_own, k.p_left, k.p_right, k.p_across, k.p_far_and_left, k.p_across_right, k.p_across_far = parts

    def return_1(k, held_back=(), held_both=()):
        back = send(after(k.p_across_far, *held_back), "right", k, "back_1_far")
        both = send(after(k.p_far_and_left, *held_both), "left", k, "back_1_both")
        k.s_across_right = plus(k.p_across_right, back)
        k.s_left = plus(k.p_left, both)
        k.s_across = plus(k.p_across, both, k.size)

    def return_2(k, held=()):
        k.s_right = plus(k.p_right, send(after(k.s_across_right, *held), "across", k, "back_2"))

    def return_3(k, held_right=(), held_left=(), held_across=()):
        k.from_left = send(after(k.s_right, *held_right), "right", k, "back_3_right")
        k.from_right = send(after(k.s_left, *held_left), "left", k, "back_3_left")
        k.from_across = send(after(k.s_across, *held_across), "across", k, "back_3_across")
        k.mixed = finish(k.state, k.span, k.p_own, k.from_left, k.from_right, k.from_across)

    def onward(k, held=()):
        k.next_state = next_section(k.mixed)
        ready = after(k.next_state, *held)
        k.next_rows = norm_call(norm_lanes_kernel, k.visit + 1, spans[k.c], ready, norm_gain, lanes)

    def made(c, visit, state, rows):
        k = Chunk()
        k.state, k.rows, k.c, k.visit = state, rows, c, visit
        k.size = sizes_of[c]
        k.span = spans[c] if visit == 0 else slice(0, k.size)
        return k

    swapped = (up_sib, down_sib)
    a = made(0, 0, activations[0], rows[0])
    b = made(1, 0, activations[0], rows[1])
    for visit in range(STOPS):
        first = visit == 0
        if first:
            gather_1(a)
            gather_2(a)
            gather_3(a)
        swap = (up_sib, down_sib,) if first else ()
        gather_1(b, ((a.left, a.right, a.across,) if first else (a.across_right,)) + swap, ((a.across_right,) if first else (a.across_right,)) + swap, ((a.far,) if first else ()) + swap)
        gather_2(b)
        gather_3(b)
        up(a, *((b.right,) if first else (b.right,)))
        down(a, *((b.pair, b.across_right,) if first else (b.pair, b.across_right,)))
        return_1(a, (b.far,), ())
        return_2(a)
        return_3(a)
        onward(a)
        up(b, *(() if first else ()))
        down(b, *((a.s_left, a.s_across,) if first else (a.s_across_right,)))
        return_1(b, () if first else (a.s_right,), () if first else ())
        return_2(b, () if first else (a.from_across,))
        if visit == STOPS - 1:
            return_3(b)
            onward(b)
            return jnp.concatenate([a.next_state, b.next_state])[None]
        c = made(0, visit + 1, a.next_state, a.next_rows)
        gather_1(c)
        gather_2(c)
        gather_3(c)
        return_3(b, (), (), ())
        onward(b, ())
        a, b = c, made(1, visit + 1, b.next_state, b.next_rows)


def solution(mesh):
    placed = (
        P("section", ("dp", "expert"), None),
        P(None, "section", ("dp", "expert"), None),
        P(None, "section", ("dp", "expert"), None),
        P("section", None),
        P("section", "expert", None, None),
        P("section", "expert", None, None),
    )
    return jax.shard_map(
        body,
        mesh=mesh,
        in_specs=placed,
        out_specs=P("section", ("dp", "expert"), None),
        check_vma=False,
    )
```
